32 devices in a mesh: groups: 2 (over x), canvas: 16 (over z, y, core).
Axes of the slice: x: 2, y: 2, z: 4, core: 2. Of those that a mesh axis runs over, the one named last changes fastest.
Arguments:
- net_slabs: int32 [65536, 2], P(('groups', 'canvas')), parts along dimension 0, may hold values from 0 to 15, all different within a row; in each aligned block of 2048 rows (0 to 2047, 2048 to 4095, ...) at most 512 rows name the same one
- row_offsets: int32 [65536, 2], P(('groups', 'canvas')), parts along dimension 0, may hold values from 0 to 15
- left_column: int32 [65536], P(('groups', 'canvas')), parts along dimension 0, may hold values from 0 to 8191
- column_span: int32 [65536], P(('groups', 'canvas')), parts along dimension 0, may hold values from 1 to 16
- pin_counts: int32 [65536], P(('groups', 'canvas')), parts along dimension 0, may hold values from 2 to 64
- tile_features: bfloat16 [7, 512, 8192], P(None, ('groups', 'canvas')), parts along dimension 1, may hold values from -6 to 6
- cotangent: float32 [512, 8192], P(('groups', 'canvas')), parts along dimension 0, may hold values from -0.0124296114 to 0.0124296114
- first_weight: bfloat16 [64, 8], replicated, may hold values from -2 to 2
- first_bias: float32 [64], replicated, may hold values from -3 to 3
- second_weight: bfloat16 [64, 64], replicated, may hold values from -0.75 to 0.75
- second_bias: float32 [64], replicated, may hold values from -3 to 3
- readout_weight: bfloat16 [64], replicated, may hold values from -0.75 to 0.75
- readout_bias: float32 [1], replicated, may hold values from -3 to 3
Outputs:
- prediction: float32 [512, 8192], P(('groups', 'canvas')), parts along dimension 0
- grad_first: float32 [128, 8], P('groups'), parts along dimension 0
- grad_first_bias: float32 [128], P('groups'), parts along dimension 0
- grad_second: float32 [128, 64], P('groups'), parts along dimension 0
- grad_second_bias: float32 [128], P('groups'), parts along dimension 0
- grad_readout: float32 [128], P('groups'), parts along dimension 0
- grad_readout_bias: float32 [2], P('groups'), parts along dimension 0
The draws below stay inside these ranges and needn't reach their ends.
There are 2 independent parts, one for each index of `groups`. The reference program is written for one: setup_inputs(seed, part) draws one part's arguments, and reference() takes and returns one part's arrays. A program takes and returns all parts, laid end to end along the dimension named above; an argument that names none is the same for every part. Nothing has to cross between parts.
Inputs may be any that keep to these rules, and one draw needn't show every extreme that they name: `net_slabs`: the two slab numbers of a net differ. Among the 2048 rows of one device no slab number is named by more than 512 rows, and in some device's rows one slab number is named by exactly 512 rows.
All inputs are finite; a program needn't handle non-finite values.
Results may differ from the reference program's by a relative error of at most 0.0071.
Values sent between devices are 32-bit elements; how exact they have to be, the bound alone decides.
A program may use at most 64 MiB of HBM per device.

```python
import math
import jax
import jax.numpy as jnp
import numpy as np
from jax import lax

ROWS_DEV = 16
W = 8192
NETS_DEV = 2048
SPAN = 16
CIN = 8
HID = 64
CF = 7
ROWS = 256
NETS = 32768
CAP = 512
N_CANVAS = 16


def draw_cotangent(key, part):
    scale = 1.0 / (ROWS * W) ** 0.5
    rising = 1.0 + 2.0 * jnp.arange(ROWS).astype(jnp.float32) / ROWS
    base = jnp.clip(jax.random.normal(key, (ROWS, W), jnp.float32), -6.0, 6.0) * scale
    return (base * rising[:, None]).astype(jnp.float32)


def set_ends(result, own_key, least, top_value):
    longest = result.shape.index(max(result.shape))
    spots = []
    for shift in (0, 1):
        where = [jax.random.randint(jax.random.fold_in(own_key, axis), (), 0, length) for axis, length in enumerate(result.shape)]
        where[longest] = (where[longest] + shift) % result.shape[longest]
        spots.append(tuple(where))
    return result.at[spots[0]].set(least).at[spots[1]].set(top_value)


def block_scale(stream_key, shape, split, smallest, largest):
    def one(dim, blocks):
        steps = jax.random.uniform(jax.random.fold_in(jax.random.fold_in(stream_key, 6), dim), (blocks,), jnp.float32, smallest / len(split), largest / len(split))
        return jnp.repeat(jnp.exp(steps), shape[dim] // blocks).reshape((-1,) + (1,) * (len(shape) - dim - 1))

    gain = one(*split[0])
    for cut in split[1:]:
        gain = gain * one(*cut)
    return gain


def deal_out(stream_key, own, number, rows, number_of, top, reach, skew):
    ranking = jax.random.permutation(stream_key, number_of)
    crowded, common = load_shares(number_of, rows * top, reach, skew, True), load_shares(number_of, rows * top, reach, skew, False)
    places = jnp.arange(number_of)

    def named(lengths, offset_by):
        used = int((lengths > 0).sum())
        fixed = max(1, used // 4)
        shifted = fixed + (places - fixed + offset_by * (used - fixed)) % max(1, number_of - fixed)
        return jnp.zeros((number_of,), jnp.int32).at[ranking[jnp.where(places < fixed, places, shifted)]].set(jnp.asarray(lengths, jnp.int32))

    lengths = jnp.where(number % 4 == 0, named(crowded, number // 4), named(common, number - number // 4 - 1))
    mixed = jax.random.permutation(jax.random.fold_in(own, 3), number_of)
    source_of, taker = mixed[0:number_of // 2 * 2:2], mixed[1:number_of // 2 * 2:2]
    margin = jnp.minimum(lengths[source_of] - 1, reach - lengths[taker]) // 2
    margin = jnp.where((source_of == ranking[0]) | (taker == ranking[0]) | (lengths[taker] == 0), 0, jnp.maximum(margin, 0))
    shifted = jax.random.randint(jax.random.fold_in(own, 4), (number_of // 2,), 0, 1 << 20) % (margin + 1)
    lengths = lengths.at[source_of].add(-shifted).at[taker].add(shifted)
    items = jnp.searchsorted(jnp.cumsum(lengths), jnp.arange(rows * top), side="right").astype(jnp.int32)
    listing = items.reshape(top, rows).T
    listing = listing[jax.random.permutation(jax.random.fold_in(own, 1), rows)]
    offset_by = jax.random.randint(jax.random.fold_in(own, 2), (rows, 1), 0, top)
    return jnp.take_along_axis(listing, (jnp.arange(top)[None, :] + offset_by) % top, axis=1)


def load_shares(amount, total, reach, lean, full):
    weights = [(1 << 20) // math.isqrt(standing ** lean) + 1 for standing in range(1, amount + 1)]
    largest = reach if full else min(reach, max(-(-total // amount), total * weights[0] // sum(weights)))
    least = 1 if total - largest >= amount - 1 else 0
    counts, surplus = [largest] + [least] * (amount - 1), total - largest - least * (amount - 1)
    while surplus > 0:
        free = [i for i in range(1, amount) if counts[i] < largest] or [i for i in range(1, amount) if counts[i] < reach]
        pool, left = sum([weights[i] for i in free]), surplus
        for i in free:
            more = min(reach - counts[i], max(1, left * weights[i] // pool), surplus)
            counts[i] = counts[i] + more
            surplus = surplus - more
    return np.array(counts)


def bell_draw(stream_key, extent, scale, bound, shards=(), dtype=jnp.bfloat16):
    values = jax.random.normal(stream_key, extent, jnp.float32) * scale
    if len(shards) > 0:
        values = block_scale(stream_key, extent, shards, -0.22, 0.18) * values
    return jnp.clip(values, min=-bound, max=bound).astype(dtype)


def setup_inputs(seed: int = 0, part: int = 0) -> dict:
    arg_keys = jax.random.split(jax.random.key(seed), 14)
    part_splits = jax.random.split(jax.random.fold_in(arg_keys[13], part), 14)
    net_slabs_keys = jax.random.split(jax.random.fold_in(part_splits[0], 1), NETS // NETS_DEV)
    net_slabs_turns = jax.random.permutation(jax.random.fold_in(part_splits[0], 3), NETS // NETS_DEV)
    net_slabs = jax.vmap(lambda own, number: deal_out(jax.random.fold_in(part_splits[0], 2), own, number, NETS_DEV, N_CANVAS, 2, CAP, 1))(net_slabs_keys, net_slabs_turns).reshape((NETS, 2))
    row_offsets = set_ends(jax.random.randint(part_splits[1], (NETS, 2), 0, ROWS_DEV), jax.random.fold_in(part_splits[1], 1), 0, ROWS_DEV - 1).astype(jnp.int32)
    left_column = set_ends(jax.random.randint(part_splits[2], (NETS,), 0, W), jax.random.fold_in(part_splits[2], 1), 0, W - 1).astype(jnp.int32)
    column_span = set_ends(jax.random.randint(part_splits[3], (NETS,), 1, SPAN + 1), jax.random.fold_in(part_splits[3], 1), 1, SPAN).astype(jnp.int32)
    pin_counts = set_ends(jax.random.randint(part_splits[4], (NETS,), 2, 65), jax.random.fold_in(part_splits[4], 1), 2, 64).astype(jnp.int32)
    tile_features = bell_draw(part_splits[5], (CF, ROWS, W), 1.0, 6.0, ((1, 16),))
    cotangent = draw_cotangent(jax.random.fold_in(jax.random.fold_in(arg_keys[13], part), 71), part)
    first_weight = bell_draw(arg_keys[7], (HID, CIN), CIN ** -0.5, 2.0)
    first_bias = bell_draw(arg_keys[8], (HID,), 0.5, 3.0, (), jnp.float32)
    second_weight = bell_draw(arg_keys[9], (HID, HID), HID ** -0.5, 0.75)
    second_bias = bell_draw(arg_keys[10], (HID,), 0.5, 3.0, (), jnp.float32)
    readout_weight = bell_draw(arg_keys[11], (HID,), HID ** -0.5, 0.75)
    readout_bias = bell_draw(arg_keys[12], (1,), 1.0, 3.0, (), jnp.float32)
    return dict(net_slabs=net_slabs, row_offsets=row_offsets, left_column=left_column, column_span=column_span, pin_counts=pin_counts, tile_features=tile_features, cotangent=cotangent, first_weight=first_weight, first_bias=first_bias, second_weight=second_weight, second_bias=second_bias, readout_weight=readout_weight, readout_bias=readout_bias)


root_half = 0.7071067811865476
inv_root_tau = 0.3989422804014327

def gelu_value(value):
    return 0.5 * value * (1.0 + jax.scipy.special.erf(value * root_half))

def gelu_slope(value):
    return 0.5 * (1.0 + jax.scipy.special.erf(value * root_half)) + value * jnp.exp(-0.5 * value * value) * inv_root_tau

def cell_block(inputs, grad_row, first_weight, first_bias, second_weight, second_bias, readout_weight, readout_bias):
    first_pre = jnp.dot(first_weight, inputs, preferred_element_type=jnp.float32) + first_bias[:, None]
    act_one = gelu_value(first_pre).astype(jnp.bfloat16)
    second_pre = jnp.dot(second_weight, act_one, preferred_element_type=jnp.float32) + second_bias[:, None]
    act_two = gelu_value(second_pre).astype(jnp.bfloat16)
    prediction = jnp.dot(readout_weight[None, :], act_two, preferred_element_type=jnp.float32)[0] + readout_bias[0]
    grad_readout = lax.optimization_barrier(jnp.sum(act_two.astype(jnp.float32) * grad_row[None, :], axis=1))
    grad_readout_bias = jnp.sum(grad_row).reshape(1)
    delta_two_full = readout_weight.astype(jnp.float32)[:, None] * grad_row[None, :] * gelu_slope(second_pre)
    delta_two = delta_two_full.astype(jnp.bfloat16)
    grad_second = jnp.dot(delta_two, act_one.T, preferred_element_type=jnp.float32)
    grad_second_bias = lax.optimization_barrier(jnp.sum(delta_two_full, axis=1))
    back_one = jnp.dot(second_weight.T, delta_two, preferred_element_type=jnp.float32)
    delta_one_full = back_one * gelu_slope(first_pre)
    delta_one = delta_one_full.astype(jnp.bfloat16)
    grad_first = jnp.dot(delta_one, inputs.T, preferred_element_type=jnp.float32)
    grad_first_bias = lax.optimization_barrier(jnp.sum(delta_one_full, axis=1))
    return (prediction, (grad_first, grad_first_bias, grad_second, grad_second_bias, grad_readout, grad_readout_bias))

def reference(net_slabs, row_offsets, left_column, column_span, pin_counts, tile_features, cotangent, first_weight, first_bias, second_weight, second_bias, readout_weight, readout_bias):
    first_is_low = net_slabs[:, 0] <= net_slabs[:, 1]
    low_slab = jnp.minimum(net_slabs[:, 0], net_slabs[:, 1])
    high_slab = jnp.maximum(net_slabs[:, 0], net_slabs[:, 1])
    low_offset = jnp.where(first_is_low, row_offsets[:, 0], row_offsets[:, 1])
    high_offset = jnp.where(first_is_low, row_offsets[:, 1], row_offsets[:, 0])
    bottom_row = (low_slab * ROWS_DEV + low_offset).astype(jnp.int32)
    top_row = (high_slab * ROWS_DEV + high_offset).astype(jnp.int32)
    right_edge = jnp.minimum(left_column + column_span, W).astype(jnp.int32)
    span_columns = (right_edge - left_column).astype(jnp.float32)
    span_rows = (top_row - bottom_row).astype(jnp.float32)
    net_weight = jnp.sqrt(pin_counts.astype(jnp.float32)) * (span_columns + span_rows) / (span_columns * span_rows)
    edges = jnp.zeros((ROWS, W + 1), jnp.float32)
    edges = edges.at[bottom_row, left_column].add(net_weight)
    edges = edges.at[bottom_row, right_edge].add(-net_weight)
    edges = edges.at[top_row, left_column].add(-net_weight)
    edges = edges.at[top_row, right_edge].add(net_weight)
    across = jnp.cumsum(edges[:, :W], axis=1)
    demand = jnp.cumsum(across, axis=0)
    level = jnp.log1p(demand).astype(jnp.bfloat16)

    def row_step(totals, row_index):
        inputs = jnp.concatenate([level[row_index][None, :], tile_features[:, row_index, :]], axis=0)
        prediction, grads = cell_block(inputs, cotangent[row_index], first_weight, first_bias, second_weight, second_bias, readout_weight, readout_bias)
        return (tuple((a + b for a, b in zip(totals, grads))), prediction)
    start = (jnp.zeros((HID, CIN), jnp.float32), jnp.zeros((HID,), jnp.float32), jnp.zeros((HID, HID), jnp.float32), jnp.zeros((HID,), jnp.float32), jnp.zeros((HID,), jnp.float32), jnp.zeros((1,), jnp.float32))
    totals, prediction = lax.scan(row_step, start, jnp.arange(ROWS).astype(jnp.int32))
    return (prediction, totals[0], totals[1], totals[2], totals[3], totals[4], totals[5])
```

```python
import functools
import jax
import jax.numpy as jnp
from jax import lax
from jax.experimental import pallas as pl
from jax.experimental.pallas import tpu as pltpu
from jax.sharding import PartitionSpec as P

root_half = 0.7071067811865476
inv_root_tau = 0.3989422804014327
log2e = 1.4426950408889634
f32 = jnp.float32
bf16 = jnp.bfloat16
i32 = jnp.int32
NT = (((1,), (1,)), ((), ()))


def iota(shape, dim):
    return lax.broadcasted_iota(i32, shape, dim)


def mlp_body(rows_per, demand_ref, base_ref, feat_ref, cot_ref, w1_ref, b1_ref, w2_ref, b2_ref, ro_ref, rb_ref,
             pred_ref, grads_ref,
             w1x, w2x, w2t, rox, col, acc1, acc2, accr, accb):
    step = pl.program_id(0)
    slab_rows, width = demand_ref.shape
    hidden, cin = w1_ref.shape
    block = rows_per * hidden
    groups = slab_rows // rows_per
    depth = (cin + 1) * slab_rows

    @pl.when(step == 0)
    def _():
        pick = (iota((block, hidden), 0) % hidden == iota((block, hidden), 1)).astype(bf16)
        pick_f = pick.astype(f32)
        spread = (iota((cin, depth), 1) // slab_rows == iota((cin, depth), 0)).astype(bf16)
        tall = jnp.dot(pick, w1_ref[...], preferred_element_type=f32).astype(bf16)
        wide = jnp.dot(tall, spread, preferred_element_type=f32)
        for g in range(groups):
            keep = (iota((block, depth), 0) // hidden + g * rows_per) == iota((block, depth), 1) % slab_rows
            w1x[g] = jnp.where(keep, wide, 0.0).astype(bf16)
        same = iota((block, block), 0) // hidden == iota((block, block), 1) // hidden
        down = jnp.dot(pick, w2_ref[...], preferred_element_type=f32).astype(bf16)
        full = lax.dot_general(down, pick, NT, preferred_element_type=f32)
        w2x[...] = jnp.where(same, full, 0.0).astype(bf16)
        flip = lax.dot_general(pick, w2_ref[...], (((1,), (1,)), ((), ())), preferred_element_type=f32).astype(bf16)
        full_t = lax.dot_general(flip, pick, NT, preferred_element_type=f32)
        w2t[...] = jnp.where(same, full_t, 0.0).astype(bf16)
        ro_wide = lax.dot_general(ro_ref[...], pick, NT, preferred_element_type=f32)
        ro_rows = jnp.broadcast_to(ro_wide, (8, block))
        rox[...] = jnp.where(iota((8, block), 0) == iota((8, block), 1) // hidden, ro_rows, 0.0).astype(bf16)
        col[0] = jnp.broadcast_to(jnp.sum(pick_f * b1_ref[...], axis=1, keepdims=True), (block, 128))
        col[1] = jnp.broadcast_to(jnp.sum(pick_f * b2_ref[...], axis=1, keepdims=True), (block, 128))
        col[2] = jnp.broadcast_to(jnp.sum(pick_f * ro_ref[...].astype(f32), axis=1, keepdims=True), (block, 128))
        acc1[...] = jnp.zeros_like(acc1)
        acc2[...] = jnp.zeros_like(acc2)
        accr[...] = jnp.zeros_like(accr)
        accb[...] = jnp.zeros_like(accb)

    level = jnp.log1p(demand_ref[...] + base_ref[...]).astype(bf16)
    feats = feat_ref[...].reshape((cin - 1) * slab_rows, width)
    ones = jnp.ones((slab_rows, width), bf16)
    x = jnp.concatenate([level, feats, ones], axis=0)
    cot = cot_ref[...]
    accb[0:slab_rows, :] += lanes(cot)
    b1 = col[0][:, 0:1]
    b2 = col[1][:, 0:1]
    ro = col[2][:, 0:1]
    for g in range(groups):
        r0 = g * rows_per
        cot_g = jnp.concatenate(
            [jnp.broadcast_to(cot[r0 + k : r0 + k + 1, :], (hidden, width)) for k in range(rows_per)], axis=0)
        v1 = jnp.dot(w1x[g], x, preferred_element_type=f32) + b1
        a1, s1 = gelu_both(v1)
        a1 = a1.astype(bf16)
        v2 = jnp.dot(w2x[...], a1, preferred_element_type=f32) + b2
        a2, s2 = gelu_both(v2)
        a2 = a2.astype(bf16)
        pred_ref[r0 : r0 + rows_per, :] = jnp.dot(rox[...], a2, preferred_element_type=f32)[0:rows_per] + rb_ref[0, 0]
        accr[...] += lanes(a2.astype(f32) * cot_g)
        d2f = (ro * cot_g) * s2
        acc_d2 = lanes(d2f)
        d2 = d2f.astype(bf16)
        accb[slab_rows : slab_rows + block, :] += acc_d2
        acc2[...] += lax.dot_general(d2, a1, NT, preferred_element_type=f32)
        back = jnp.dot(w2t[...], d2, preferred_element_type=f32)
        d1 = (back * s1).astype(bf16)
        acc1[g] += lax.dot_general(d1, x, NT, preferred_element_type=f32)

    @pl.when(step == pl.num_programs(0) - 1)
    def _():
        def fold(a):
            return sum(a[k * hidden : (k + 1) * hidden] for k in range(rows_per))

        total2 = acc2[...]
        g2 = sum(total2[k * hidden : (k + 1) * hidden, k * hidden : (k + 1) * hidden] for k in range(rows_per))
        total1 = jnp.zeros((hidden, depth), f32)
        for g in range(groups):
            keep = (iota((block, depth), 0) // hidden + g * rows_per) == iota((block, depth), 1) % slab_rows
            total1 += fold(jnp.where(keep, acc1[g], 0.0))
        gather = (iota((depth, hidden), 0) // slab_rows == iota((depth, hidden), 1)).astype(f32)
        g1 = jnp.dot(total1, gather, precision=lax.Precision.HIGHEST, preferred_element_type=f32)
        gr = fold(jnp.sum(accr[...], axis=1, keepdims=True))
        gb2 = fold(jnp.sum(accb[slab_rows : slab_rows + block, :], axis=1, keepdims=True))
        gb3 = jnp.sum(accb[0:slab_rows, :], keepdims=True)
        lane = iota((hidden, hidden), 1)
        right = jnp.where(lane == cin + 1, gr, jnp.where(lane == cin + 2, gb2, jnp.where(lane == cin + 3, gb3, g1)))
        packed = jnp.concatenate([g2, right], axis=1)
        n, k, _ = grads_ref.shape
        for j in range(n):
            grads_ref[j] = packed[j * k : (j + 1) * k]


def lanes(a):
    return sum(a[:, k * 128 : (k + 1) * 128] for k in range(a.shape[1] // 128))


def gelu_both(v):
    w = v * root_half
    phi = 0.5 + 0.5 * lax.erf(w)
    bell = jnp.exp2((w * w) * (-log2e))
    return v * phi, phi + (v * inv_root_tau) * bell


def mlp(demand, base, feats, cot, w1, b1, w2, b2, ro, rb, devices, rows_per=4, width=1024):
    slab_rows, w = demand.shape
    hidden, cin = w1.shape
    block = rows_per * hidden
    depth = (cin + 1) * slab_rows
    whole = lambda s: pl.BlockSpec(s, lambda i: tuple(0 for _ in s))
    cols = pl.BlockSpec((slab_rows, width), lambda i: (0, i))
    return pl.pallas_call(
        functools.partial(mlp_body, rows_per),
        grid=(w // width,),
        in_specs=[
            cols, pl.BlockSpec((1, width), lambda i: (0, i)),
            pl.BlockSpec((cin - 1, slab_rows, width), lambda i: (0, 0, i)), cols,
            whole((hidden, cin)), whole((1, hidden)), whole((hidden, hidden)), whole((1, hidden)), whole((1, hidden)),
            pl.BlockSpec(memory_space=pltpu.SMEM),
        ],
        out_specs=[cols, whole((devices, hidden // devices, 2 * hidden))],
        out_shape=[
            jax.ShapeDtypeStruct((slab_rows, w), f32),
            jax.ShapeDtypeStruct((devices, hidden // devices, 2 * hidden), f32),
        ],
        scratch_shapes=[
            pltpu.VMEM((slab_rows // rows_per, block, depth), bf16),
            pltpu.VMEM((block, block), bf16),
            pltpu.VMEM((block, block), bf16),
            pltpu.VMEM((8, block), bf16),
            pltpu.VMEM((3, block, 128), f32),
            pltpu.VMEM((slab_rows // rows_per, block, depth), f32),
            pltpu.VMEM((block, block), f32),
            pltpu.VMEM((block, 128), f32),
            pltpu.VMEM((slab_rows + block, 128), f32),
        ],
        name="mlp",
    )(demand, base, feats, cot, w1, b1[None, :], w2, b2[None, :], ro[None, :], rb[None, :])


def greet(n):
    me, group = lax.axis_index("canvas"), lax.axis_index("groups")
    barrier = pltpu.get_barrier_semaphore()

    def hail(k, carry):
        pl.semaphore_signal(
            barrier, inc=1, device_id=(group, lax.rem(me + k, n)), device_id_type=pl.DeviceIdType.MESH)
        return carry

    lax.fori_loop(1, n, hail, 0)
    pl.semaphore_wait(barrier, n - 1)


def swap(n, source, target, send_sem, recv_sem):
    me, group = lax.axis_index("canvas"), lax.axis_index("groups")

    def copy(k, slot):
        peer = lax.rem(me + k, n)
        return pltpu.make_async_remote_copy(
            src_ref=source.at[peer], dst_ref=target.at[slot], send_sem=send_sem.at[k], recv_sem=recv_sem.at[k],
            device_id=(group, peer), device_id_type=pl.DeviceIdType.MESH)

    def start(k, carry):
        copy(k, me).start()
        return carry

    def arrive(k, carry):
        copy(k, lax.rem(me + n - k, n)).wait_recv()
        return carry

    lax.fori_loop(1, n, start, 0)
    target[pl.ds(me, 1)] = source[pl.ds(me, 1)]
    lax.fori_loop(1, n, arrive, 0)

    def finish():
        def left(k, carry):
            copy(k, me).wait_send()
            return carry

        lax.fori_loop(1, n, left, 0)

    return finish


def items_body(n, send_ref, got_ref, send_sem, recv_sem):
    greet(n)
    swap(n, send_ref, got_ref, send_sem, recv_sem)()


def base_body(n, totals_ref, base_ref, got, result, back, send_a, recv_a, send_b, recv_b):
    greet(n)
    end_a = swap(n, totals_ref, got, send_a, recv_a)
    running = jnp.zeros(got.shape[1:], f32)
    for d in range(n):
        result[d] = running
        running = running + got[d]
    end_b = swap(n, result, back, send_b, recv_b)
    part = got.shape[2]
    for d in range(n):
        base_ref[:, d * part : (d + 1) * part] = back[d]
    end_a()
    end_b()


def sum_body(n, grads_ref, out_ref, got, result, back, send_a, recv_a, send_b, recv_b):
    greet(n)
    end_a = swap(n, grads_ref, got, send_a, recv_a)
    total = got[0]
    for d in range(1, n):
        total = total + got[d]
    for d in range(n):
        result[d] = total
    end_b = swap(n, result, back, send_b, recv_b)
    k = got.shape[1]
    for d in range(n):
        out_ref[d * k : (d + 1) * k, :] = back[d]
    end_a()
    end_b()


def linked(body, n, x, out_shape, phases, collective_id, name):
    vmem = pl.BlockSpec(memory_space=pltpu.VMEM)
    extra = [pltpu.VMEM(x.shape, f32)] * 3 if phases == 2 else []
    return pl.pallas_call(
        functools.partial(body, n),
        out_shape=jax.ShapeDtypeStruct(out_shape, f32),
        in_specs=[vmem],
        out_specs=vmem,
        scratch_shapes=extra + [pltpu.SemaphoreType.DMA((n,))] * (2 * phases),
        compiler_params=pltpu.CompilerParams(collective_id=collective_id, has_side_effects=True),
        name=name,
    )(x)


def slab_body(lane_group, got_ref, local_ref, totals_ref, acc):
    n, _, cap = got_ref.shape
    slab_rows, w = local_ref.shape
    tail = 128
    per = max(1, min(n, 2048 // cap))
    for c in range(n // per):
        def line(which):
            return jnp.concatenate([got_ref[c * per + j, which : which + 1, :] for j in range(per)], axis=1)

        value = line(0)
        place = line(1).astype(i32)
        end = line(2).astype(i32)
        row = place // w
        start = place - row * w
        group = start // lane_group
        first = start - group * lane_group
        last = end - group * lane_group
        key = group * slab_rows + row
        limit = (group + 1) * slab_rows
        hi = value.astype(bf16).astype(f32)
        lo = value - hi
        count = per * cap
        m = iota((acc.shape[0], count), 0)
        hot = jnp.where((m >= key) & (m < limit), 1.0, 0.0).astype(bf16)
        lane = iota((lane_group, count), 0)
        inside = (lane >= first) & (lane < last)
        over = (iota((tail, count), 0) + lane_group) < last
        fine = jnp.concatenate(
            [jnp.where(inside, hi, 0.0).astype(bf16), jnp.where(inside, lo, 0.0).astype(bf16),
             jnp.where(over, hi, 0.0).astype(bf16), jnp.where(over, lo, 0.0).astype(bf16)], axis=0)
        update = lax.dot_general(hot, fine, NT, preferred_element_type=f32)
        if c == 0:
            acc[...] = update
        else:
            acc[...] += update
    g2 = 2 * lane_group
    for q in range(w // lane_group):
        rows = slice(q * slab_rows, (q + 1) * slab_rows)
        main = acc[rows, 0:lane_group] + acc[rows, lane_group:g2]
        local_ref[:, q * lane_group : (q + 1) * lane_group] = main
        if q > 0:
            before = slice((q - 1) * slab_rows, q * slab_rows)
            spill = acc[before, g2 : g2 + tail] + acc[before, g2 + tail : g2 + 2 * tail]
            local_ref[:, q * lane_group : q * lane_group + tail] = main[:, 0:tail] + spill
    part = w // n
    for d in range(n):
        totals_ref[d] = local_ref[slab_rows - 1 : slab_rows, d * part : (d + 1) * part]


def slab(got, slab_rows, w, lane_group=256):
    n = got.shape[0]
    return pl.pallas_call(
        functools.partial(slab_body, lane_group),
        out_shape=[jax.ShapeDtypeStruct((slab_rows, w), f32), jax.ShapeDtypeStruct((n, 1, w // n), f32)],
        in_specs=[pl.BlockSpec(memory_space=pltpu.VMEM)],
        out_specs=[pl.BlockSpec(memory_space=pltpu.VMEM)] * 2,
        scratch_shapes=[pltpu.VMEM((slab_rows * w // lane_group, 2 * lane_group + 256), f32)],
        name="slab",
    )(got)


def per_device(
    net_slabs,
    row_offsets,
    left_column,
    column_span,
    pin_counts,
    tile_features,
    cotangent,
    first_weight,
    first_bias,
    second_weight,
    second_bias,
    readout_weight,
    readout_bias,
):
    devices = lax.axis_size("canvas")
    slab_rows = tile_features.shape[1]
    canvas_width = tile_features.shape[2]
    nets_here = pin_counts.shape[0]
    capacity = 4 * nets_here // devices
    highest = lax.Precision.HIGHEST
    first_is_low = net_slabs[:, 0] <= net_slabs[:, 1]
    low_slab = jnp.minimum(net_slabs[:, 0], net_slabs[:, 1])
    high_slab = jnp.maximum(net_slabs[:, 0], net_slabs[:, 1])
    low_offset = jnp.where(first_is_low, row_offsets[:, 0], row_offsets[:, 1])
    high_offset = jnp.where(first_is_low, row_offsets[:, 1], row_offsets[:, 0])
    right_edge = jnp.minimum(left_column + column_span, canvas_width)
    span_columns = (right_edge - left_column).astype(jnp.float32)
    span_rows = ((high_slab - low_slab) * slab_rows + high_offset - low_offset).astype(jnp.float32)
    net_weight = (
        jnp.sqrt(pin_counts.astype(jnp.float32))
        * (span_columns + span_rows)
        / (span_columns * span_rows)
    )
    target_slab = jnp.concatenate([low_slab, high_slab])
    local_row = jnp.concatenate([low_offset, high_offset])
    start_column = jnp.concatenate([left_column, left_column])
    end_column = jnp.concatenate([right_edge, right_edge])
    amounts = jnp.concatenate([net_weight, -net_weight])
    item_count = target_slab.shape[0]
    slab_ids = jnp.arange(devices, dtype=jnp.int32)
    slab_hot = (target_slab[:, None] == slab_ids[None, :]).astype(jnp.bfloat16)
    block_len = 128
    block_count = item_count // block_len
    blocked_hot = slab_hot.reshape(block_count, block_len, devices)
    lower_ones = (jnp.arange(block_len)[:, None] >= jnp.arange(block_len)[None, :]).astype(
        jnp.bfloat16
    )
    inclusive = jnp.einsum(
        "ij,bjd->bid", lower_ones, blocked_hot, preferred_element_type=jnp.float32
    )
    block_totals = inclusive[:, -1, :]
    block_start = jnp.cumsum(block_totals, axis=0) - block_totals
    counted = (inclusive + block_start[:, None, :] - 1.0) * blocked_hot.astype(jnp.float32)
    slot_rank = jnp.sum(counted, axis=2).reshape(item_count).astype(jnp.int32)
    payload = jnp.stack(
        [
            amounts,
            (local_row * canvas_width + start_column).astype(jnp.float32),
            end_column.astype(jnp.float32),
        ]
    )
    dest_mask = (slab_ids[:, None] == target_slab[None, :]).astype(jnp.float32)
    left_side = (dest_mask[:, None, :] * payload[None, :, :]).reshape(3 * devices, item_count)
    rank_hot = (slot_rank[:, None] == jnp.arange(capacity, dtype=jnp.int32)[None, :]).astype(
        jnp.float32
    )
    send_items = jnp.dot(
        left_side, rank_hot, precision=highest, preferred_element_type=jnp.float32
    ).reshape(devices, 3, capacity)
    got_items = linked(items_body, devices, send_items, send_items.shape, 1, 0, "items")
    local, totals = slab(got_items, slab_rows, canvas_width)
    base = linked(base_body, devices, totals, (1, canvas_width), 2, 1, "base")
    prediction, grads = mlp(
        local, base, tile_features, cotangent, first_weight, first_bias, second_weight, second_bias,
        readout_weight, readout_bias, devices)
    hidden, cin = first_weight.shape
    summed = linked(sum_body, devices, grads, (hidden, 2 * hidden), 2, 2, "sum")
    right = summed[:, hidden:]
    return (prediction, right[:, :cin], right[:, cin], summed[:, :hidden], right[:, cin + 2], right[:, cin + 1],
            right[0:1, cin + 3])


def solution(mesh):
    in_specs = (
        P(("groups", "canvas"), None),
        P(("groups", "canvas"), None),
        P(("groups", "canvas")),
        P(("groups", "canvas")),
        P(("groups", "canvas")),
        P(None, ("groups", "canvas"), None),
        P(("groups", "canvas"), None),
        P(),
        P(),
        P(),
        P(),
        P(),
        P(),
    )
    out_specs = (
        P(("groups", "canvas"), None),
        P("groups", None),
        P("groups"),
        P("groups", None),
        P("groups"),
        P("groups"),
        P("groups"),
    )
    return jax.shard_map(
        per_device, mesh=mesh, in_specs=in_specs, out_specs=out_specs, check_vma=False
    )
```

```python
import functools
import jax
import jax.numpy as jnp
from jax import lax
from jax.experimental import pallas as pl
from jax.experimental.pallas import tpu as pltpu
from jax.sharding import PartitionSpec as P

root_half = 0.7071067811865476
inv_root_tau = 0.3989422804014327
log2e = 1.4426950408889634
f32 = jnp.float32
bf16 = jnp.bfloat16
i32 = jnp.int32
NT = (((1,), (1,)), ((), ()))


def iota(shape, dim):
    return lax.broadcasted_iota(i32, shape, dim)


def mlp_body(rows_per, demand_ref, base_ref, feat_ref, cot_ref, w1_ref, b1_ref, w2_ref, b2_ref, ro_ref, rb_ref,
             pred_ref, grads_ref,
             w1x, w2x, w2t, rox, col, acc1, acc2, accr, accb):
    step = pl.program_id(0)
    slab_rows, width = demand_ref.shape
    hidden, cin = w1_ref.shape
    block = rows_per * hidden
    groups = slab_rows // rows_per
    depth = (cin + 1) * slab_rows

    @pl.when(step == 0)
    def _():
        pick = (iota((block, hidden), 0) % hidden == iota((block, hidden), 1)).astype(bf16)
        pick_f = pick.astype(f32)
        spread = (iota((cin, depth), 1) // slab_rows == iota((cin, depth), 0)).astype(bf16)
        tall = jnp.dot(pick, w1_ref[...], preferred_element_type=f32).astype(bf16)
        wide = jnp.dot(tall, spread, preferred_element_type=f32)
        for g in range(groups):
            keep = (iota((block, depth), 0) // hidden + g * rows_per) == iota((block, depth), 1) % slab_rows
            w1x[g] = jnp.where(keep, wide, 0.0).astype(bf16)
        same = iota((block, block), 0) // hidden == iota((block, block), 1) // hidden
        down = jnp.dot(pick, w2_ref[...], preferred_element_type=f32).astype(bf16)
        full = lax.dot_general(down, pick, NT, preferred_element_type=f32)
        w2x[...] = jnp.where(same, full, 0.0).astype(bf16)
        flip = lax.dot_general(pick, w2_ref[...], (((1,), (1,)), ((), ())), preferred_element_type=f32).astype(bf16)
        full_t = lax.dot_general(flip, pick, NT, preferred_element_type=f32)
        w2t[...] = jnp.where(same, full_t, 0.0).astype(bf16)
        ro_wide = lax.dot_general(ro_ref[...], pick, NT, preferred_element_type=f32)
        ro_rows = jnp.broadcast_to(ro_wide, (8, block))
        rox[...] = jnp.where(iota((8, block), 0) == iota((8, block), 1) // hidden, ro_rows, 0.0).astype(bf16)
        col[0] = jnp.broadcast_to(jnp.sum(pick_f * b1_ref[...], axis=1, keepdims=True), (block, 128))
        col[1] = jnp.broadcast_to(jnp.sum(pick_f * b2_ref[...], axis=1, keepdims=True), (block, 128))
        col[2] = jnp.broadcast_to(jnp.sum(pick_f * ro_ref[...].astype(f32), axis=1, keepdims=True), (block, 128))
        acc1[...] = jnp.zeros_like(acc1)
        acc2[...] = jnp.zeros_like(acc2)
        accr[...] = jnp.zeros_like(accr)
        accb[...] = jnp.zeros_like(accb)

    level = jnp.log1p(demand_ref[...] + base_ref[...]).astype(bf16)
    feats = feat_ref[...].reshape((cin - 1) * slab_rows, width)
    ones = jnp.ones((slab_rows, width), bf16)
    x = jnp.concatenate([level, feats, ones], axis=0)
    cot = cot_ref[...]
    accb[0:slab_rows, :] += lanes(cot)
    b1 = col[0][:, 0:1]
    b2 = col[1][:, 0:1]
    ro = col[2][:, 0:1]
    for g in range(groups):
        r0 = g * rows_per
        cot_g = jnp.concatenate(
            [jnp.broadcast_to(cot[r0 + k : r0 + k + 1, :], (hidden, width)) for k in range(rows_per)], axis=0)
        v1 = jnp.dot(w1x[g], x, preferred_element_type=f32) + b1
        a1, s1 = gelu_both(v1)
        a1 = a1.astype(bf16)
        v2 = jnp.dot(w2x[...], a1, preferred_element_type=f32) + b2
        a2, s2 = gelu_both(v2)
        a2 = a2.astype(bf16)
        pred_ref[r0 : r0 + rows_per, :] = jnp.dot(rox[...], a2, preferred_element_type=f32)[0:rows_per] + rb_ref[0, 0]
        accr[...] += lanes(a2.astype(f32) * cot_g)
        d2f = (ro * cot_g) * s2
        acc_d2 = lanes(d2f)
        d2 = d2f.astype(bf16)
        accb[slab_rows : slab_rows + block, :] += acc_d2
        acc2[...] += lax.dot_general(d2, a1, NT, preferred_element_type=f32)
        back = jnp.dot(w2t[...], d2, preferred_element_type=f32)
        d1 = (back * s1).astype(bf16)
        acc1[g] += lax.dot_general(d1, x, NT, preferred_element_type=f32)

    @pl.when(step == pl.num_programs(0) - 1)
    def _():
        def fold(a):
            return sum(a[k * hidden : (k + 1) * hidden] for k in range(rows_per))

        total2 = acc2[...]
        g2 = sum(total2[k * hidden : (k + 1) * hidden, k * hidden : (k + 1) * hidden] for k in range(rows_per))
        total1 = jnp.zeros((hidden, depth), f32)
        for g in range(groups):
            keep = (iota((block, depth), 0) // hidden + g * rows_per) == iota((block, depth), 1) % slab_rows
            total1 += fold(jnp.where(keep, acc1[g], 0.0))
        gather = (iota((depth, hidden), 0) // slab_rows == iota((depth, hidden), 1)).astype(f32)
        g1 = jnp.dot(total1, gather, precision=lax.Precision.HIGHEST, preferred_element_type=f32)
        gr = fold(jnp.sum(accr[...], axis=1, keepdims=True))
        gb2 = fold(jnp.sum(accb[slab_rows : slab_rows + block, :], axis=1, keepdims=True))
        gb3 = jnp.sum(accb[0:slab_rows, :], keepdims=True)
        lane = iota((hidden, hidden), 1)
        right = jnp.where(lane == cin + 1, gr, jnp.where(lane == cin + 2, gb2, jnp.where(lane == cin + 3, gb3, g1)))
        packed = jnp.concatenate([g2, right], axis=1)
        n, k, _ = grads_ref.shape
        for j in range(n):
            grads_ref[j] = packed[j * k : (j + 1) * k]


def lanes(a):
    return sum(a[:, k * 128 : (k + 1) * 128] for k in range(a.shape[1] // 128))


def gelu_both(v):
    w = v * root_half
    phi = 0.5 + 0.5 * lax.erf(w)
    bell = jnp.exp2((w * w) * (-log2e))
    return v * phi, phi + (v * inv_root_tau) * bell


def mlp(demand, base, feats, cot, w1, b1, w2, b2, ro, rb, devices, rows_per=4, width=1024):
    slab_rows, w = demand.shape
    hidden, cin = w1.shape
    block = rows_per * hidden
    depth = (cin + 1) * slab_rows
    whole = lambda s: pl.BlockSpec(s, lambda i: tuple(0 for _ in s))
    cols = pl.BlockSpec((slab_rows, width), lambda i: (0, i))
    return pl.pallas_call(
        functools.partial(mlp_body, rows_per),
        grid=(w // width,),
        in_specs=[
            cols, pl.BlockSpec((1, width), lambda i: (0, i)),
            pl.BlockSpec((cin - 1, slab_rows, width), lambda i: (0, 0, i)), cols,
            whole((hidden, cin)), whole((1, hidden)), whole((hidden, hidden)), whole((1, hidden)), whole((1, hidden)),
            pl.BlockSpec(memory_space=pltpu.SMEM),
        ],
        out_specs=[cols, whole((devices, hidden // devices, 2 * hidden))],
        out_shape=[
            jax.ShapeDtypeStruct((slab_rows, w), f32),
            jax.ShapeDtypeStruct((devices, hidden // devices, 2 * hidden), f32),
        ],
        scratch_shapes=[
            pltpu.VMEM((slab_rows // rows_per, block, depth), bf16),
            pltpu.VMEM((block, block), bf16),
            pltpu.VMEM((block, block), bf16),
            pltpu.VMEM((8, block), bf16),
            pltpu.VMEM((3, block, 128), f32),
            pltpu.VMEM((slab_rows // rows_per, block, depth), f32),
            pltpu.VMEM((block, block), f32),
            pltpu.VMEM((block, 128), f32),
            pltpu.VMEM((slab_rows + block, 128), f32),
        ],
        name="mlp",
    )(demand, base, feats, cot, w1, b1[None, :], w2, b2[None, :], ro[None, :], rb[None, :])


def greet(n):
    me, group = lax.axis_index("canvas"), lax.axis_index("groups")
    barrier = pltpu.get_barrier_semaphore()

    def hail(k, carry):
        pl.semaphore_signal(
            barrier, inc=1, device_id=(group, lax.rem(me + k, n)), device_id_type=pl.DeviceIdType.MESH)
        return carry

    lax.fori_loop(1, n, hail, 0)
    pl.semaphore_wait(barrier, n - 1)


def swap(n, source, target, send_sem, recv_sem):
    me, group = lax.axis_index("canvas"), lax.axis_index("groups")

    def copy(k, slot):
        peer = lax.rem(me + k, n)
        return pltpu.make_async_remote_copy(
            src_ref=source.at[peer], dst_ref=target.at[slot], send_sem=send_sem.at[k], recv_sem=recv_sem.at[k],
            device_id=(group, peer), device_id_type=pl.DeviceIdType.MESH)

    def start(k, carry):
        copy(k, me).start()
        return carry

    def arrive(k, carry):
        copy(k, lax.rem(me + n - k, n)).wait_recv()
        return carry

    lax.fori_loop(1, n, start, 0)
    target[pl.ds(me, 1)] = source[pl.ds(me, 1)]
    lax.fori_loop(1, n, arrive, 0)

    def finish():
        def left(k, carry):
            copy(k, me).wait_send()
            return carry

        lax.fori_loop(1, n, left, 0)

    return finish


def route_body(n, lane_group, send_ref, local_ref, base_ref, items, acc, totals, got, result, back,
               send_a, recv_a, send_b, recv_b, send_c, recv_c):
    greet(n)
    end_a = swap(n, send_ref, items, send_a, recv_a)
    slab(lane_group, items, local_ref, totals, acc)
    end_b = swap(n, totals, got, send_b, recv_b)
    running = jnp.zeros(got.shape[1:], f32)
    for d in range(n):
        result[d] = running
        running = running + got[d]
    end_c = swap(n, result, back, send_c, recv_c)
    part = got.shape[2]
    for d in range(n):
        base_ref[:, d * part : (d + 1) * part] = back[d]
    end_a()
    end_b()
    end_c()


def route(send, slab_rows, w, lane_group=256):
    n = send.shape[0]
    vmem = pl.BlockSpec(memory_space=pltpu.VMEM)
    part = pltpu.VMEM((n, 1, w // n), f32)
    return pl.pallas_call(
        functools.partial(route_body, n, lane_group),
        out_shape=[jax.ShapeDtypeStruct((slab_rows, w), f32), jax.ShapeDtypeStruct((1, w), f32)],
        in_specs=[vmem],
        out_specs=[vmem] * 2,
        scratch_shapes=[
            pltpu.VMEM(send.shape, f32), pltpu.VMEM((slab_rows * w // lane_group, 2 * lane_group + 256), f32),
            part, part, part, part,
        ] + [pltpu.SemaphoreType.DMA((n,))] * 6,
        compiler_params=pltpu.CompilerParams(collective_id=0, has_side_effects=True),
        name="route",
    )(send)


def sum_body(n, grads_ref, g1_ref, gb1_ref, g2_ref, gb2_ref, gr_ref, gb_ref, got, result, back, total_ref,
             send_a, recv_a, send_b, recv_b):
    greet(n)
    end_a = swap(n, grads_ref, got, send_a, recv_a)
    total = got[0]
    for d in range(1, n):
        total = total + got[d]
    for d in range(n):
        result[d] = total
    end_b = swap(n, result, back, send_b, recv_b)
    k = got.shape[1]
    for d in range(n):
        total_ref[d * k : (d + 1) * k, :] = back[d]
    hidden, cin = g1_ref.shape
    g2_ref[...] = total_ref[:, 0:hidden]
    right = total_ref[:, hidden:]
    g1_ref[...] = right[:, 0:cin]
    eye = iota((hidden, hidden), 0) == iota((hidden, hidden), 1)

    def row(lane):
        return jnp.sum(jnp.where(eye, right[:, lane : lane + 1], 0.0), axis=0, keepdims=True)

    gb1_ref[...] = row(cin)
    gr_ref[...] = row(cin + 1)
    gb2_ref[...] = row(cin + 2)
    gb_ref[...] = right[0:1, cin + 3 : cin + 4]
    end_a()
    end_b()


def sum_all(grads, cin):
    n, k, _ = grads.shape
    hidden = n * k
    vmem = pl.BlockSpec(memory_space=pltpu.VMEM)
    line = (1, hidden)
    return pl.pallas_call(
        functools.partial(sum_body, n),
        out_shape=[
            jax.ShapeDtypeStruct(shape, f32)
            for shape in ((hidden, cin), line, (hidden, hidden), line, line, (1, 1))
        ],
        in_specs=[vmem],
        out_specs=[vmem] * 6,
        scratch_shapes=[pltpu.VMEM(grads.shape, f32)] * 3
        + [pltpu.VMEM((hidden, 2 * hidden), f32)]
        + [pltpu.SemaphoreType.DMA((n,))] * 4,
        compiler_params=pltpu.CompilerParams(collective_id=1, has_side_effects=True),
        name="sum_all",
    )(grads)


def slab(lane_group, got_ref, local_ref, totals_ref, acc):
    n, _, cap = got_ref.shape
    slab_rows, w = local_ref.shape
    tail = 128
    per = max(1, min(n, 2048 // cap))
    for c in range(n // per):
        def line(which):
            return jnp.concatenate([got_ref[c * per + j, which : which + 1, :] for j in range(per)], axis=1)

        value = line(0)
        place = line(1).astype(i32)
        end = line(2).astype(i32)
        row = place // w
        start = place - row * w
        group = start // lane_group
        first = start - group * lane_group
        last = end - group * lane_group
        key = group * slab_rows + row
        limit = (group + 1) * slab_rows
        hi = value.astype(bf16).astype(f32)
        lo = value - hi
        count = per * cap
        m = iota((acc.shape[0], count), 0)
        hot = jnp.where((m >= key) & (m < limit), 1.0, 0.0).astype(bf16)
        lane = iota((lane_group, count), 0)
        inside = (lane >= first) & (lane < last)
        over = (iota((tail, count), 0) + lane_group) < last
        fine = jnp.concatenate(
            [jnp.where(inside, hi, 0.0).astype(bf16), jnp.where(inside, lo, 0.0).astype(bf16),
             jnp.where(over, hi, 0.0).astype(bf16), jnp.where(over, lo, 0.0).astype(bf16)], axis=0)
        update = lax.dot_general(hot, fine, NT, preferred_element_type=f32)
        if c == 0:
            acc[...] = update
        else:
            acc[...] += update
    g2 = 2 * lane_group
    for q in range(w // lane_group):
        rows = slice(q * slab_rows, (q + 1) * slab_rows)
        main = acc[rows, 0:lane_group] + acc[rows, lane_group:g2]
        local_ref[:, q * lane_group : (q + 1) * lane_group] = main
        if q > 0:
            before = slice((q - 1) * slab_rows, q * slab_rows)
            spill = acc[before, g2 : g2 + tail] + acc[before, g2 + tail : g2 + 2 * tail]
            local_ref[:, q * lane_group : q * lane_group + tail] = main[:, 0:tail] + spill
    part = w // n
    for d in range(n):
        totals_ref[d] = local_ref[slab_rows - 1 : slab_rows, d * part : (d + 1) * part]


def per_device(
    net_slabs,
    row_offsets,
    left_column,
    column_span,
    pin_counts,
    tile_features,
    cotangent,
    first_weight,
    first_bias,
    second_weight,
    second_bias,
    readout_weight,
    readout_bias,
):
    devices = lax.axis_size("canvas")
    slab_rows = tile_features.shape[1]
    canvas_width = tile_features.shape[2]
    nets_here = pin_counts.shape[0]
    capacity = 4 * nets_here // devices
    first_is_low = net_slabs[:, 0] <= net_slabs[:, 1]
    low_slab = jnp.minimum(net_slabs[:, 0], net_slabs[:, 1])
    high_slab = jnp.maximum(net_slabs[:, 0], net_slabs[:, 1])
    low_offset = jnp.where(first_is_low, row_offsets[:, 0], row_offsets[:, 1])
    high_offset = jnp.where(first_is_low, row_offsets[:, 1], row_offsets[:, 0])
    right_edge = jnp.minimum(left_column + column_span, canvas_width)
    span_columns = (right_edge - left_column).astype(jnp.float32)
    span_rows = ((high_slab - low_slab) * slab_rows + high_offset - low_offset).astype(jnp.float32)
    net_weight = (
        jnp.sqrt(pin_counts.astype(jnp.float32))
        * (span_columns + span_rows)
        / (span_columns * span_rows)
    )
    target_slab = jnp.concatenate([low_slab, high_slab])
    local_row = jnp.concatenate([low_offset, high_offset])
    start_column = jnp.concatenate([left_column, left_column])
    end_column = jnp.concatenate([right_edge, right_edge])
    amounts = jnp.concatenate([net_weight, -net_weight])
    item_count = target_slab.shape[0]
    slab_ids = jnp.arange(devices, dtype=jnp.int32)
    slab_hot = (target_slab[:, None] == slab_ids[None, :]).astype(jnp.bfloat16)
    block_len = 128
    block_count = item_count // block_len
    blocked_hot = slab_hot.reshape(block_count, block_len, devices)
    lower_ones = (jnp.arange(block_len)[:, None] >= jnp.arange(block_len)[None, :]).astype(
        jnp.bfloat16
    )
    inclusive = jnp.einsum(
        "ij,bjd->bid", lower_ones, blocked_hot, preferred_element_type=jnp.float32
    )
    block_totals = inclusive[:, -1, :]
    block_start = jnp.cumsum(block_totals, axis=0) - block_totals
    counted = (inclusive + block_start[:, None, :] - 1.0) * blocked_hot.astype(jnp.float32)
    slot_rank = jnp.sum(counted, axis=2).reshape(item_count).astype(jnp.int32)
    high_amounts = lax.reduce_precision(amounts, 8, 7)
    fine = 64
    terms = jnp.stack(
        [
            high_amounts,
            amounts - high_amounts,
            local_row.astype(jnp.float32),
            (start_column // fine).astype(jnp.float32),
            (start_column % fine).astype(jnp.float32),
            (end_column - start_column).astype(jnp.float32),
        ]
    ).astype(jnp.bfloat16)
    dest_mask = (slab_ids[:, None] == target_slab[None, :]).astype(jnp.bfloat16)
    left_side = (terms[:, None, :] * dest_mask[None, :, :]).reshape(6 * devices, item_count)
    rank_hot = (slot_rank[:, None] == jnp.arange(capacity, dtype=jnp.int32)[None, :]).astype(
        jnp.bfloat16
    )
    placed = jnp.dot(left_side, rank_hot, preferred_element_type=jnp.float32).reshape(6, devices, capacity)
    first = placed[3] * fine + placed[4]
    send_items = jnp.stack(
        [placed[0] + placed[1], placed[2] * canvas_width + first, first + placed[5]], axis=1
    )
    local, base = route(send_items, slab_rows, canvas_width)
    prediction, grads = mlp(
        local, base, tile_features, cotangent, first_weight, first_bias, second_weight, second_bias,
        readout_weight, readout_bias, devices)
    g1, gb1, g2, gb2, gr, gb = sum_all(grads, first_weight.shape[1])
    return (prediction, g1, gb1[0], g2, gb2[0], gr[0], gb[0])


def solution(mesh):
    in_specs = (
        P(("groups", "canvas"), None),
        P(("groups", "canvas"), None),
        P(("groups", "canvas")),
        P(("groups", "canvas")),
        P(("groups", "canvas")),
        P(None, ("groups", "canvas"), None),
        P(("groups", "canvas"), None),
        P(),
        P(),
        P(),
        P(),
        P(),
        P(),
    )
    out_specs = (
        P(("groups", "canvas"), None),
        P("groups", None),
        P("groups"),
        P("groups", None),
        P("groups"),
        P("groups"),
        P("groups"),
    )
    return jax.shard_map(
        per_device, mesh=mesh, in_specs=in_specs, out_specs=out_specs, check_vma=False
    )
```

```python
import functools
import jax
import jax.numpy as jnp
from jax import lax
from jax.experimental import pallas as pl
from jax.experimental.pallas import tpu as pltpu
from jax.sharding import PartitionSpec as P

root_half = 0.7071067811865476
inv_root_tau = 0.3989422804014327
log2e = 1.4426950408889634
f32 = jnp.float32
bf16 = jnp.bfloat16
i32 = jnp.int32
NARROW = (False, False)
NT = (((1,), (1,)), ((), ()))


def iota(shape, dim):
    return lax.broadcasted_iota(i32, shape, dim)


def mlp_body(rows_per, demand_ref, base_ref, feat_ref, cot_ref, w1_ref, b1_ref, w2_ref, b2_ref, ro_ref, rb_ref,
             pred_ref, grads_ref,
             w1x, w2x, w2t, rox, col, acc1, acc2, accr, accb):
    step = pl.program_id(0)
    slab_rows, width = demand_ref.shape
    hidden, cin = w1_ref.shape
    block = rows_per * hidden
    groups = slab_rows // rows_per
    depth = (cin + 1) * slab_rows

    @pl.when(step == 0)
    def _():
        pick = (iota((block, hidden), 0) % hidden == iota((block, hidden), 1)).astype(bf16)
        pick_f = pick.astype(f32)
        spread = (iota((cin, depth), 1) // slab_rows == iota((cin, depth), 0)).astype(bf16)
        tall = jnp.dot(pick, w1_ref[...], preferred_element_type=f32).astype(bf16)
        wide = jnp.dot(tall, spread, preferred_element_type=f32)
        for g in range(groups):
            keep = (iota((block, depth), 0) // hidden + g * rows_per) == iota((block, depth), 1) % slab_rows
            w1x[g] = jnp.where(keep, wide, 0.0).astype(bf16)
        same = iota((block, block), 0) // hidden == iota((block, block), 1) // hidden
        down = jnp.dot(pick, w2_ref[...], preferred_element_type=f32).astype(bf16)
        full = lax.dot_general(down, pick, NT, preferred_element_type=f32)
        w2x[...] = jnp.where(same, 0.5 * full, 0.0).astype(bf16)
        flip = lax.dot_general(pick, w2_ref[...], (((1,), (1,)), ((), ())), preferred_element_type=f32).astype(bf16)
        full_t = lax.dot_general(flip, pick, NT, preferred_element_type=f32)
        w2t[...] = jnp.where(same, 0.5 * full_t, 0.0).astype(bf16)
        ro_wide = lax.dot_general(ro_ref[...], pick, NT, preferred_element_type=f32)
        ro_rows = jnp.broadcast_to(ro_wide, (8, block))
        rox[...] = jnp.where(iota((8, block), 0) == iota((8, block), 1) // hidden, 0.5 * ro_rows, 0.0).astype(bf16)
        col[0] = jnp.broadcast_to(jnp.sum(pick_f * b1_ref[...], axis=1, keepdims=True), (block, 128))
        col[1] = jnp.broadcast_to(jnp.sum(pick_f * b2_ref[...], axis=1, keepdims=True), (block, 128))
        col[2] = 0.5 * jnp.broadcast_to(jnp.sum(pick_f * ro_ref[...].astype(f32), axis=1, keepdims=True), (block, 128))
        acc1[...] = jnp.zeros_like(acc1)
        acc2[...] = jnp.zeros_like(acc2)
        accr[...] = jnp.zeros_like(accr)
        accb[...] = jnp.zeros_like(accb)

    level = jnp.log1p(demand_ref[...] + base_ref[...]).astype(bf16)
    feats = feat_ref[...].reshape((cin - 1) * slab_rows, width)
    ones = jnp.ones((slab_rows, width), bf16)
    x = jnp.concatenate([level, feats, ones], axis=0)
    cot = cot_ref[...]
    accb[0:slab_rows, :] += lanes(cot)
    b1 = col[0][:, 0:1]
    b2 = col[1][:, 0:1]
    ro = col[2][:, 0:1]
    for g in range(groups):
        r0 = g * rows_per
        cot_g = jnp.concatenate(
            [jnp.broadcast_to(cot[r0 + k : r0 + k + 1, :], (hidden, width)) for k in range(rows_per)], axis=0)
        v1 = jnp.dot(w1x[g], x, preferred_element_type=f32) + b1
        a1, s1 = gelu_twice(v1, NARROW[0])
        a1 = a1.astype(bf16)
        v2 = jnp.dot(w2x[...], a1, preferred_element_type=f32) + b2
        a2, s2 = gelu_twice(v2, NARROW[1])
        a2 = a2.astype(bf16)
        pred_ref[r0 : r0 + rows_per, :] = jnp.dot(rox[...], a2, preferred_element_type=f32)[0:rows_per] + rb_ref[0, 0]
        accr[...] += lanes(a2.astype(f32) * cot_g)
        d2f = (ro * cot_g) * s2
        acc_d2 = lanes(d2f)
        d2 = d2f.astype(bf16)
        accb[slab_rows : slab_rows + block, :] += acc_d2
        acc2[...] += lax.dot_general(d2, a1, NT, preferred_element_type=f32)
        back = jnp.dot(w2t[...], d2, preferred_element_type=f32)
        d1 = (back * s1).astype(bf16)
        acc1[g] += lax.dot_general(d1, x, NT, preferred_element_type=f32)

    @pl.when(step == pl.num_programs(0) - 1)
    def _():
        def fold(a):
            return sum(a[k * hidden : (k + 1) * hidden] for k in range(rows_per))

        total2 = acc2[...]
        g2 = 0.5 * sum(total2[k * hidden : (k + 1) * hidden, k * hidden : (k + 1) * hidden] for k in range(rows_per))
        total1 = jnp.zeros((hidden, depth), f32)
        for g in range(groups):
            keep = (iota((block, depth), 0) // hidden + g * rows_per) == iota((block, depth), 1) % slab_rows
            total1 += fold(jnp.where(keep, acc1[g], 0.0))
        gather = (iota((depth, hidden), 0) // slab_rows == iota((depth, hidden), 1)).astype(f32)
        g1 = jnp.dot(total1, gather, precision=lax.Precision.HIGHEST, preferred_element_type=f32)
        gr = 0.5 * fold(jnp.sum(accr[...], axis=1, keepdims=True))
        gb2 = fold(jnp.sum(accb[slab_rows : slab_rows + block, :], axis=1, keepdims=True))
        gb3 = jnp.sum(accb[0:slab_rows, :], keepdims=True)
        lane = iota((hidden, hidden), 1)
        right = jnp.where(lane == cin + 1, gr, jnp.where(lane == cin + 2, gb2, jnp.where(lane == cin + 3, gb3, g1)))
        packed = jnp.concatenate([g2, right], axis=1)
        n, k, _ = grads_ref.shape
        for j in range(n):
            grads_ref[j] = packed[j * k : (j + 1) * k]


def lanes(a):
    return sum(a[:, k * 128 : (k + 1) * 128] for k in range(a.shape[1] // 128))


def gelu_twice(v, narrow):
    w = v * root_half
    if narrow:
        w = w.astype(bf16)
        tail = (v * (2.0 * inv_root_tau)).astype(bf16)
        bell = jnp.exp2((w * w) * bf16(-log2e))
        both = 1.0 + lax.erf(w).astype(f32)
        return v * both, both + (tail * bell).astype(f32)
    both = 1.0 + lax.erf(w)
    bell = jnp.exp2((w * w) * (-log2e))
    return v * both, both + (v * (2.0 * inv_root_tau)) * bell


def mlp(demand, base, feats, cot, w1, b1, w2, b2, ro, rb, devices, rows_per=4, width=1024):
    slab_rows, w = demand.shape
    hidden, cin = w1.shape
    block = rows_per * hidden
    depth = (cin + 1) * slab_rows
    whole = lambda s: pl.BlockSpec(s, lambda i: tuple(0 for _ in s))
    cols = pl.BlockSpec((slab_rows, width), lambda i: (0, i))
    return pl.pallas_call(
        functools.partial(mlp_body, rows_per),
        grid=(w // width,),
        in_specs=[
            cols, pl.BlockSpec((1, width), lambda i: (0, i)),
            pl.BlockSpec((cin - 1, slab_rows, width), lambda i: (0, 0, i)), cols,
            whole((hidden, cin)), whole((1, hidden)), whole((hidden, hidden)), whole((1, hidden)), whole((1, hidden)),
            pl.BlockSpec(memory_space=pltpu.SMEM),
        ],
        out_specs=[cols, whole((devices, hidden // devices, 2 * hidden))],
        out_shape=[
            jax.ShapeDtypeStruct((slab_rows, w), f32),
            jax.ShapeDtypeStruct((devices, hidden // devices, 2 * hidden), f32),
        ],
        scratch_shapes=[
            pltpu.VMEM((slab_rows // rows_per, block, depth), bf16),
            pltpu.VMEM((block, block), bf16),
            pltpu.VMEM((block, block), bf16),
            pltpu.VMEM((8, block), bf16),
            pltpu.VMEM((3, block, 128), f32),
            pltpu.VMEM((slab_rows // rows_per, block, depth), f32),
            pltpu.VMEM((block, block), f32),
            pltpu.VMEM((block, 128), f32),
            pltpu.VMEM((slab_rows + block, 128), f32),
        ],
        name="mlp",
    )(demand, base, feats, cot, w1, b1[None, :], w2, b2[None, :], ro[None, :], rb[None, :])


def greet(n):
    me, group = lax.axis_index("canvas"), lax.axis_index("groups")
    barrier = pltpu.get_barrier_semaphore()

    def hail(k, carry):
        pl.semaphore_signal(
            barrier, inc=1, device_id=(group, lax.rem(me + k, n)), device_id_type=pl.DeviceIdType.MESH)
        return carry

    lax.fori_loop(1, n, hail, 0)
    pl.semaphore_wait(barrier, n - 1)


def swap(n, source, target, send_sem, recv_sem):
    me, group = lax.axis_index("canvas"), lax.axis_index("groups")

    def copy(k, slot):
        peer = lax.rem(me + k, n)
        return pltpu.make_async_remote_copy(
            src_ref=source.at[peer], dst_ref=target.at[slot], send_sem=send_sem.at[k], recv_sem=recv_sem.at[k],
            device_id=(group, peer), device_id_type=pl.DeviceIdType.MESH)

    def start(k, carry):
        copy(k, me).start()
        return carry

    def arrive(k, carry):
        copy(k, lax.rem(me + n - k, n)).wait_recv()
        return carry

    lax.fori_loop(1, n, start, 0)
    target[pl.ds(me, 1)] = source[pl.ds(me, 1)]
    lax.fori_loop(1, n, arrive, 0)

    def finish():
        def left(k, carry):
            copy(k, me).wait_send()
            return carry

        lax.fori_loop(1, n, left, 0)

    return finish


def route_body(n, lane_group, send_ref, local_ref, base_ref, items, acc, totals, got, result, back,
               send_a, recv_a, send_b, recv_b, send_c, recv_c):
    greet(n)
    end_a = swap(n, send_ref, items, send_a, recv_a)
    slab(lane_group, items, local_ref, totals, acc)
    end_b = swap(n, totals, got, send_b, recv_b)
    running = jnp.zeros(got.shape[1:], f32)
    for d in range(n):
        result[d] = running
        running = running + got[d]
    end_c = swap(n, result, back, send_c, recv_c)
    part = got.shape[2]
    for d in range(n):
        base_ref[:, d * part : (d + 1) * part] = back[d]
    end_a()
    end_b()
    end_c()


def route(send, slab_rows, w, lane_group=256):
    n = send.shape[0]
    vmem = pl.BlockSpec(memory_space=pltpu.VMEM)
    part = pltpu.VMEM((n, 1, w // n), f32)
    return pl.pallas_call(
        functools.partial(route_body, n, lane_group),
        out_shape=[jax.ShapeDtypeStruct((slab_rows, w), f32), jax.ShapeDtypeStruct((1, w), f32)],
        in_specs=[vmem],
        out_specs=[vmem] * 2,
        scratch_shapes=[
            pltpu.VMEM(send.shape, f32), pltpu.VMEM((slab_rows * w // lane_group, 2 * lane_group + 256), f32),
            part, part, part, part,
        ] + [pltpu.SemaphoreType.DMA((n,))] * 6,
        compiler_params=pltpu.CompilerParams(collective_id=0, has_side_effects=True),
        name="route",
    )(send)


def sum_body(n, grads_ref, total_ref, got, result, back, send_a, recv_a, send_b, recv_b):
    greet(n)
    end_a = swap(n, grads_ref, got, send_a, recv_a)
    total = got[0]
    for d in range(1, n):
        total = total + got[d]
    for d in range(n):
        result[d] = total
    end_b = swap(n, result, back, send_b, recv_b)
    k = got.shape[1]
    for d in range(n):
        total_ref[d * k : (d + 1) * k, :] = back[d]
    end_a()
    end_b()


def split_body(total_ref, g1_out, gb1_out, g2_out, gb2_out, gr_out, gb_out,
               g1_ref, gb1_ref, g2_ref, gb2_ref, gr_ref, gb_ref, out_sem):
    cin, hidden = g1_ref.shape
    g2_ref[...] = total_ref[:, 0:hidden]
    right = total_ref[:, hidden:]
    eye = iota((hidden, hidden), 0) == iota((hidden, hidden), 1)

    def row(lane):
        return jnp.sum(jnp.where(eye, right[:, lane : lane + 1], 0.0), axis=0, keepdims=True)

    g1_ref[...] = jnp.concatenate([row(c) for c in range(cin)], axis=0)
    gb1_ref[...] = row(cin).reshape(hidden)
    gr_ref[...] = row(cin + 1).reshape(hidden)
    gb2_ref[...] = row(cin + 2).reshape(hidden)
    gb_ref[...] = right[0:1, cin + 3 : cin + 4].reshape(1)
    pairs = ((g1_ref, g1_out), (gb1_ref, gb1_out), (g2_ref, g2_out), (gb2_ref, gb2_out), (gr_ref, gr_out),
             (gb_ref, gb_out))
    copies = [pltpu.make_async_copy(source, target, out_sem.at[i]) for i, (source, target) in enumerate(pairs)]
    for c in copies:
        c.start()
    for c in copies:
        c.wait()


def sum_all(grads, cin):
    n, k, _ = grads.shape
    hidden = n * k
    vmem = pl.BlockSpec(memory_space=pltpu.VMEM)
    line = (hidden,)
    shapes = ((cin, hidden), line, (hidden, hidden), line, line, (1,))
    total = linked(sum_body, n, grads, (hidden, 2 * hidden), 2, 1, "sum_all")
    return pl.pallas_call(
        split_body,
        out_shape=[jax.ShapeDtypeStruct(shape, f32) for shape in shapes],
        in_specs=[vmem],
        out_specs=[pl.BlockSpec(memory_space=pltpu.HBM)] * 6,
        scratch_shapes=[pltpu.VMEM(shape, f32) for shape in shapes] + [pltpu.SemaphoreType.DMA((6,))],
        name="split",
    )(total)


def linked(body, n, x, out_shape, phases, collective_id, name):
    vmem = pl.BlockSpec(memory_space=pltpu.VMEM)
    extra = [pltpu.VMEM(x.shape, f32)] * 3 if phases == 2 else []
    return pl.pallas_call(
        functools.partial(body, n),
        out_shape=jax.ShapeDtypeStruct(out_shape, f32),
        in_specs=[vmem],
        out_specs=vmem,
        scratch_shapes=extra + [pltpu.SemaphoreType.DMA((n,))] * (2 * phases),
        compiler_params=pltpu.CompilerParams(collective_id=collective_id, has_side_effects=True),
        name=name,
    )(x)


def slab(lane_group, got_ref, local_ref, totals_ref, acc):
    n, _, cap = got_ref.shape
    slab_rows, w = local_ref.shape
    tail = 128
    per = max(1, min(n, 2048 // cap))
    for c in range(n // per):
        def line(which):
            return jnp.concatenate([got_ref[c * per + j, which : which + 1, :] for j in range(per)], axis=1)

        value = line(0)
        place = line(1).astype(i32)
        end = line(2).astype(i32)
        row = place // w
        start = place - row * w
        group = start // lane_group
        first = start - group * lane_group
        last = end - group * lane_group
        key = group * slab_rows + row
        limit = (group + 1) * slab_rows
        hi = value.astype(bf16).astype(f32)
        lo = value - hi
        count = per * cap
        m = iota((acc.shape[0], count), 0)
        hot = jnp.where((m >= key) & (m < limit), 1.0, 0.0).astype(bf16)
        lane = iota((lane_group, count), 0)
        inside = (lane >= first) & (lane < last)
        over = (iota((tail, count), 0) + lane_group) < last
        fine = jnp.concatenate(
            [jnp.where(inside, hi, 0.0).astype(bf16), jnp.where(inside, lo, 0.0).astype(bf16),
             jnp.where(over, hi, 0.0).astype(bf16), jnp.where(over, lo, 0.0).astype(bf16)], axis=0)
        update = lax.dot_general(hot, fine, NT, preferred_element_type=f32)
        if c == 0:
            acc[...] = update
        else:
            acc[...] += update
    g2 = 2 * lane_group
    for q in range(w // lane_group):
        rows = slice(q * slab_rows, (q + 1) * slab_rows)
        main = acc[rows, 0:lane_group] + acc[rows, lane_group:g2]
        local_ref[:, q * lane_group : (q + 1) * lane_group] = main
        if q > 0:
            before = slice((q - 1) * slab_rows, q * slab_rows)
            spill = acc[before, g2 : g2 + tail] + acc[before, g2 + tail : g2 + 2 * tail]
            local_ref[:, q * lane_group : q * lane_group + tail] = main[:, 0:tail] + spill
    part = w // n
    for d in range(n):
        totals_ref[d] = local_ref[slab_rows - 1 : slab_rows, d * part : (d + 1) * part]


def per_device(
    net_slabs,
    row_offsets,
    left_column,
    column_span,
    pin_counts,
    tile_features,
    cotangent,
    first_weight,
    first_bias,
    second_weight,
    second_bias,
    readout_weight,
    readout_bias,
):
    devices = lax.axis_size("canvas")
    slab_rows = tile_features.shape[1]
    canvas_width = tile_features.shape[2]
    nets_here = pin_counts.shape[0]
    capacity = 4 * nets_here // devices
    first_is_low = net_slabs[:, 0] <= net_slabs[:, 1]
    low_slab = jnp.minimum(net_slabs[:, 0], net_slabs[:, 1])
    high_slab = jnp.maximum(net_slabs[:, 0], net_slabs[:, 1])
    low_offset = jnp.where(first_is_low, row_offsets[:, 0], row_offsets[:, 1])
    high_offset = jnp.where(first_is_low, row_offsets[:, 1], row_offsets[:, 0])
    right_edge = jnp.minimum(left_column + column_span, canvas_width)
    span_columns = (right_edge - left_column).astype(jnp.float32)
    span_rows = ((high_slab - low_slab) * slab_rows + high_offset - low_offset).astype(jnp.float32)
    net_weight = (
        jnp.sqrt(pin_counts.astype(jnp.float32))
        * (span_columns + span_rows)
        / (span_columns * span_rows)
    )
    target_slab = jnp.concatenate([low_slab, high_slab])
    local_row = jnp.concatenate([low_offset, high_offset])
    start_column = jnp.concatenate([left_column, left_column])
    end_column = jnp.concatenate([right_edge, right_edge])
    amounts = jnp.concatenate([net_weight, -net_weight])
    item_count = target_slab.shape[0]
    highest = lax.Precision.HIGHEST
    slab_ids = jnp.arange(devices, dtype=jnp.int32)
    slab_hot = (target_slab[:, None] == slab_ids[None, :]).astype(jnp.bfloat16)
    block_len = 128
    block_count = item_count // block_len
    blocked_hot = slab_hot.reshape(block_count, block_len, devices)
    lower_ones = (jnp.arange(block_len)[:, None] >= jnp.arange(block_len)[None, :]).astype(
        jnp.bfloat16
    )
    inclusive = jnp.einsum(
        "ij,bjd->bid", lower_ones, blocked_hot, preferred_element_type=jnp.float32
    )
    block_totals = inclusive[:, -1, :]
    block_start = jnp.cumsum(block_totals, axis=0) - block_totals
    counted = (inclusive + block_start[:, None, :] - 1.0) * blocked_hot.astype(jnp.float32)
    slot_rank = jnp.sum(counted, axis=2).reshape(item_count).astype(jnp.int32)
    payload = jnp.stack(
        [
            amounts,
            (local_row * canvas_width + start_column).astype(jnp.float32),
            end_column.astype(jnp.float32),
        ]
    )
    dest_mask = (slab_ids[:, None] == target_slab[None, :]).astype(jnp.float32)
    left_side = (dest_mask[:, None, :] * payload[None, :, :]).reshape(3 * devices, item_count)
    rank_hot = (slot_rank[:, None] == jnp.arange(capacity, dtype=jnp.int32)[None, :]).astype(
        jnp.float32
    )
    send_items = jnp.dot(
        left_side, rank_hot, precision=highest, preferred_element_type=jnp.float32
    ).reshape(devices, 3, capacity)
    local, base = route(send_items, slab_rows, canvas_width)
    prediction, grads = mlp(
        local, base, tile_features, cotangent, first_weight, first_bias, second_weight, second_bias,
        readout_weight, readout_bias, devices)
    g1, gb1, g2, gb2, gr, gb = sum_all(grads, first_weight.shape[1])
    return (prediction, g1.T, gb1, g2, gb2, gr, gb)


def solution(mesh):
    in_specs = (
        P(("groups", "canvas"), None),
        P(("groups", "canvas"), None),
        P(("groups", "canvas")),
        P(("groups", "canvas")),
        P(("groups", "canvas")),
        P(None, ("groups", "canvas"), None),
        P(("groups", "canvas"), None),
        P(),
        P(),
        P(),
        P(),
        P(),
        P(),
    )
    out_specs = (
        P(("groups", "canvas"), None),
        P("groups", None),
        P("groups"),
        P("groups", None),
        P("groups"),
        P("groups"),
        P("groups"),
    )
    return jax.shard_map(
        per_device, mesh=mesh, in_specs=in_specs, out_specs=out_specs, check_vma=False
    )
```
